32 devices in a mesh: cfg: 2 (over core), tm: 2 (over x), space: 8 (over z, y).
Axes of the slice: x: 2, y: 2, z: 4, core: 2. Of those that a mesh axis runs over, the one named last changes fastest.
Arguments:
- solutions: bfloat16 [4, 2, 3, 1024, 384], P(('cfg', 'tm'), None, None, 'space'), parts along dimension 0, may hold values from -6 to 6
- eigvecs: bfloat16 [4, 2, 3, 1024, 384], P(('cfg', 'tm'), None, None, 'space'), parts along dimension 0, may hold values from -0.078125 to 0.078125
- meson: bfloat16 [4, 4, 2, 384, 384], P(None, ('cfg', 'tm')), parts along dimension 1, may hold values from -0.015625 to 0.015625
- momenta: int32 [4, 3], replicated, may hold values from -3 to 3
- source_time: int32 [384], replicated, may hold values from 0 to 1
- dilution: int32 [384], replicated, may hold values from 0 to 3
Outputs:
- blocks: float32 [4, 2, 384, 4, 384], P(None, None, ('tm', 'space'), 'cfg'), parts along dimension 3
The draws below stay inside these ranges and needn't reach their ends.
There are 2 independent parts, one for each index of `cfg`. The reference program is written for one: setup_inputs(seed, part) draws one part's arguments, and reference() takes and returns one part's arrays. A program takes and returns all parts, laid end to end along the dimension named above; an argument that names none is the same for every part. Nothing has to cross between parts.
All inputs are finite; a program needn't handle non-finite values.
Results may differ from the reference program's by a relative error of at most 0.0056.
Values may be sent and summed in bfloat16 or wider, within the bound.
A program may use at most 64 MiB of HBM per device.

```python
import jax
import jax.numpy as jnp
from jax import lax

SIDE = 48
NEV = 384
NCOL = 384
MOMENTA = 4
NDIL = 4
XS = 1024
NT = 2


def plant(result, stream_key, smallest, high):
    spot = [jax.random.randint(jax.random.fold_in(stream_key, axis), (), 0, length) for axis, length in enumerate(result.shape)]
    longest = result.shape.index(max(result.shape))
    beside = spot[:longest] + [(spot[longest] + 1) % result.shape[longest]] + spot[longest + 1:]
    return result.at[tuple(spot)].set(smallest).at[tuple(beside)].set(high)


def shard_levels(own_key, shape, split, smallest, top_value):
    def one(axis_at, blocks):
        draws = jax.random.uniform(jax.random.fold_in(jax.random.fold_in(own_key, 6), axis_at), (blocks,), jnp.float32, smallest / len(split), top_value / len(split))
        return jnp.repeat(jnp.exp(draws), shape[axis_at] // blocks).reshape((-1,) + (1,) * (len(shape) - axis_at - 1))

    gain = one(*split[0])
    for cut in split[1:]:
        gain = gain * one(*cut)
    return gain


def bell_draw(key, extent, width, most, shards=(), held_as=jnp.bfloat16):
    level = shard_levels(key, extent, shards, -0.22, 0.18) if shards else 1.0
    array = jax.random.normal(key, extent, jnp.float32) * width * level
    return jnp.minimum(jnp.maximum(array, -most), most).astype(held_as)


def setup_inputs(seed: int = 0, part: int = 0) -> dict:
    key_of = jax.random.split(jax.random.key(seed), 7)
    part_splits = jax.random.split(jax.random.fold_in(key_of[6], part), 7)
    return {
        "solutions": bell_draw(part_splits[0], (NT, 2, 3, XS, NCOL), 1.0, 6.0, ((0, 2), (3, 8))),
        "eigvecs": bell_draw(part_splits[1], (NT, 2, 3, XS, NEV), (6 * XS) ** -0.5, 0.078125, ((0, 2), (3, 8))),
        "meson": bell_draw(part_splits[2], (MOMENTA, NT, 2, NEV, NEV), (NEV * NEV) ** -0.5, 0.015625, ((1, 2),)),
        "momenta": plant(jax.random.randint(key_of[3], (MOMENTA, 3), -3, 4), jax.random.fold_in(key_of[3], 1), -3, 3).astype(jnp.int32),
        "source_time": plant(jax.random.randint(key_of[4], (NCOL,), 0, NT), jax.random.fold_in(key_of[4], 1), 0, NT - 1).astype(jnp.int32),
        "dilution": plant(jax.random.randint(key_of[5], (NCOL,), 0, NDIL), jax.random.fold_in(key_of[5], 1), 0, NDIL - 1).astype(jnp.int32),
    }


def contract(first_op, second_op):
    return lax.dot_general(first_op, second_op, (((0,), (0,)), ((), ())), preferred_element_type=jnp.float32)


def reference(solutions, eigvecs, meson, momenta, source_time, dilution):
    site_index = jnp.arange(XS, dtype=jnp.int32)
    coordinates = jnp.stack([site_index % SIDE, (site_index // SIDE) % SIDE, site_index // (SIDE * SIDE)], 0)
    windings = jnp.sum(momenta[:, :, None] * coordinates[None], 1)
    angles = (2.0 * jnp.pi / SIDE) * windings.astype(jnp.float32)
    cosine = jnp.cos(angles)[:, None, :, None]
    sine_part = jnp.sin(angles)[:, None, :, None]

    def project(inputs):
        solution, vectors = inputs
        solve_real = solution[0].astype(jnp.float32)
        solve_imag = solution[1].astype(jnp.float32)
        phased_real = cosine * solve_real[None] + sine_part * solve_imag[None]
        phased_imag = cosine * solve_imag[None] - sine_part * solve_real[None]
        phased_real = jnp.moveaxis(phased_real, 0, -1).reshape(3 * XS, NCOL * MOMENTA).astype(jnp.bfloat16)
        phased_imag = jnp.moveaxis(phased_imag, 0, -1).reshape(3 * XS, NCOL * MOMENTA).astype(jnp.bfloat16)
        base_real = solution[0].reshape(3 * XS, NCOL)
        base_imag = solution[1].reshape(3 * XS, NCOL)
        vec_real = vectors[0].reshape(3 * XS, NEV)
        vec_imag = vectors[1].reshape(3 * XS, NEV)
        zero_real = contract(base_real, vec_real) + contract(base_imag, vec_imag)
        zero_imag = contract(base_imag, vec_real) - contract(base_real, vec_imag)
        mom_real = contract(phased_real, vec_real) + contract(phased_imag, vec_imag)
        mom_imag = contract(phased_imag, vec_real) - contract(phased_real, vec_imag)
        zero_mom = jnp.stack([zero_real, zero_imag], 1)[:, None]
        momentum = jnp.stack([mom_real, mom_imag], 1).reshape(NCOL, MOMENTA, 2, NEV)
        return jnp.concatenate([zero_mom, momentum], 1)

    coefficients = lax.map(project, (solutions, eigvecs)).astype(jnp.bfloat16)
    dilution_mask = ((jnp.arange(NEV, dtype=jnp.int32) % NDIL)[None, :] == dilution[:, None]).astype(jnp.bfloat16)
    zero_mom = coefficients[:, :, 0] * dilution_mask[None, :, None, :]
    momentum = coefficients[:, :, 1:]
    meson_real = meson[:, :, 0].astype(jnp.float32)
    meson_imag = meson[:, :, 1].astype(jnp.float32)
    coef_real = momentum[:, :, :, 0].astype(jnp.float32)
    coef_imag = momentum[:, :, :, 1].astype(jnp.float32)
    left_real = (jnp.einsum('tapk,ptkl->ptal', coef_real, meson_real) + jnp.einsum('tapk,ptkl->ptal', coef_imag, meson_imag)).astype(jnp.bfloat16).astype(jnp.float32)
    left_imag = (jnp.einsum('tapk,ptkl->ptal', coef_real, meson_imag) - jnp.einsum('tapk,ptkl->ptal', coef_imag, meson_real)).astype(jnp.bfloat16).astype(jnp.float32)
    zero_real = zero_mom[:, :, 0].astype(jnp.float32)
    zero_imag = zero_mom[:, :, 1].astype(jnp.float32)
    pair_real = jnp.einsum('ptal,tbl->ptab', left_real, zero_real) - jnp.einsum('ptal,tbl->ptab', left_imag, zero_imag)
    pair_imag = jnp.einsum('ptal,tbl->ptab', left_real, zero_imag) + jnp.einsum('ptal,tbl->ptab', left_imag, zero_real)
    offsets = (source_time[:, None] + jnp.arange(NT, dtype=jnp.int32)[None, :]) % NT
    selector = (offsets[:, :, None] == jnp.arange(NT, dtype=jnp.int32)[None, None, :]).astype(jnp.float32)
    result_real = jnp.einsum('adt,ptab->padb', selector, pair_real, precision=lax.Precision.HIGHEST)
    result_imag = jnp.einsum('adt,ptab->padb', selector, pair_imag, precision=lax.Precision.HIGHEST)
    return jnp.stack([result_real, result_imag], 1)
```

```python
import functools

import jax
import jax.numpy as jnp
import numpy as np
from jax import lax
from jax.experimental import pallas as pl
from jax.experimental.pallas import tpu as pltpu
from jax.sharding import PartitionSpec as P

SIDE = 48
NDIL = 4
MESH = pl.DeviceIdType.MESH
F32 = jnp.float32
BF16 = jnp.bfloat16


def dot(a, b, dims=((1,), (0,))):
    return lax.dot_general(a, b, (dims, ((), ())), preferred_element_type=F32)


def kernel(
    zc, tc,
    sol_ref, eig_ref, meson_hbm, cos_ref, sin_ref, dst_ref, dil_ref,
    out_ref,
    meson, solt, lhs, ysend, yrecv, own, zsend, zrecv, osend,
    q_y, q_yr, q_z, q_zr, q_f, q_fr, zfull, xrecv,
    meson_sem, ys, yr, zs, zr, xs, xr, qys, qyr, qzs, qzr, qfs, qfr,
):
    moments = cos_ref.shape[0]
    depth, cols = sol_ref.shape
    vecs = eig_ref.shape[1]
    half = cols // 2
    flat = depth // 2
    chunk = half // zc
    cl = chunk // tc
    small = vecs // NDIL

    s = lax.axis_index("space")
    t = lax.axis_index("tm")
    y = s % 2
    z = s // 2
    ypeer = {"space": z * 2 + (1 - y)}

    def zpeer(i):
        return {"space": ((z + i) % zc) * 2 + y}

    def xpeer(i):
        return (t + i) % tc

    def y_copy(p):
        return pltpu.make_async_remote_copy(
            src_ref=ysend.at[p], dst_ref=yrecv.at[p], send_sem=ys.at[p], recv_sem=yr.at[p],
            device_id=ypeer, device_id_type=MESH)

    def z_copy(p, i):
        return pltpu.make_async_remote_copy(
            src_ref=zsend.at[p, (z + i) % zc], dst_ref=zrecv.at[p, i - 1],
            send_sem=zs.at[p, i - 1], recv_sem=zr.at[p, i - 1],
            device_id=zpeer(i), device_id_type=MESH)

    def x_copy(p, i):
        return pltpu.make_async_remote_copy(
            src_ref=osend.at[p, xpeer(i)], dst_ref=xrecv.at[p, t],
            send_sem=xs.at[p, i - 1], recv_sem=xr.at[p, i - 1],
            device_id={"tm": xpeer(i)}, device_id_type=MESH)

    def qy_copy():
        return pltpu.make_async_remote_copy(
            src_ref=q_y.at[1 - y], dst_ref=q_yr, send_sem=qys, recv_sem=qyr,
            device_id=ypeer, device_id_type=MESH)

    def qz_copy(i):
        return pltpu.make_async_remote_copy(
            src_ref=q_z, dst_ref=q_zr.at[i - 1], send_sem=qzs.at[i - 1], recv_sem=qzr.at[i - 1],
            device_id=zpeer(i), device_id_type=MESH)

    def qf_copy():
        return pltpu.make_async_remote_copy(
            src_ref=q_f, dst_ref=q_fr, send_sem=qfs, recv_sem=qfr,
            device_id=ypeer, device_id_type=MESH)

    meson_copy = pltpu.make_async_copy(meson_hbm, meson, meson_sem)
    meson_copy.start()

    barrier = pltpu.get_barrier_semaphore()
    pl.semaphore_signal(barrier, inc=1, device_id=ypeer, device_id_type=MESH)
    for i in range(1, zc):
        pl.semaphore_signal(barrier, inc=1, device_id=zpeer(i), device_id_type=MESH)
    for i in range(1, tc):
        pl.semaphore_signal(barrier, inc=1, device_id={"tm": xpeer(i)}, device_id_type=MESH)

    sol = sol_ref[...]
    eig = eig_ref[...]
    turned = jnp.concatenate([sol[flat:], -sol[:flat]], 0)
    k_row = lax.broadcasted_iota(jnp.int32, (vecs, cols), 0)
    keep = (k_row & (NDIL - 1)) == dil_ref[...]
    j_row = lax.broadcasted_iota(jnp.int32, (small, vecs), 0) * NDIL
    k_col = lax.broadcasted_iota(jnp.int32, (small, vecs), 1)
    gather = ((k_col >= j_row) & (k_col < j_row + NDIL)).astype(F32).astype(BF16)
    for part, rhs in enumerate((sol, turned)):
        full = dot(eig, rhs, ((0,), (0,)))
        full = jnp.where(keep, full, 0.0).astype(BF16)
        q_y[part] = dot(gather, full).astype(BF16)

    c_row = lax.broadcasted_iota(jnp.int32, (cols, cols), 0)
    perm = (c_row == dst_ref[...]).astype(F32).astype(BF16)
    moved = dot(perm, sol, ((1,), (1,)))
    solt[0] = moved[:half]
    solt[1] = moved[half:]

    pl.semaphore_wait(barrier, 1 + (zc - 1) + (tc - 1))
    qy_copy().start()

    def partial(p, which):
        block = solt[which]
        re, im = block[:, :flat], block[:, flat:]
        c, sn = cos_ref[p], sin_ref[p]
        pr = (c * re + sn * im).astype(BF16)
        pi = (c * im - sn * re).astype(BF16)
        lhs[:half, :flat] = pr
        lhs[:half, flat:] = pi
        lhs[half:, :flat] = pi
        lhs[half:, flat:] = -pr
        return dot(lhs[...], eig_ref[...])

    def send_other(p, carry):
        ysend[p] = partial(p, 1 - y).astype(BF16)
        y_copy(p).start()
        return carry

    lax.fori_loop(0, moments, send_other, 0)

    qy_copy().wait_recv()
    q_z[...] = (q_y[y].astype(F32) + q_yr[...].astype(F32)).astype(BF16)
    for i in range(1, zc):
        qz_copy(i).start()

    def keep_own(p, carry):
        own[p] = partial(p, y)
        return carry

    lax.fori_loop(0, moments, keep_own, 0)

    for i in range(1, zc):
        qz_copy(i).wait_recv()
    total = q_z[...].astype(F32)
    for i in range(1, zc):
        total = total + q_zr[i - 1].astype(F32)
    q_f[...] = total.astype(BF16)
    qf_copy().start()

    def scatter(p):
        y_copy(p).wait_recv()
        summed = (own[p] + yrecv[p].astype(F32)).astype(BF16)
        for c in range(zc):
            for part in range(2):
                first = part * half + c * chunk
                zsend[p, c, part] = summed[first:first + chunk]
        for i in range(1, zc):
            z_copy(p, i).start()

    def finish(p):
        coef = zsend[p, z].astype(F32)
        for i in range(1, zc):
            z_copy(p, i).wait_recv()
            coef = coef + zrecv[p, i - 1].astype(F32)
        coef = coef.astype(BF16)
        cr, ci = coef[0], coef[1]
        left = dot(
            jnp.concatenate(
                [jnp.concatenate([cr, ci], 1), jnp.concatenate([-ci, cr], 1)], 0),
            meson[p]).astype(BF16)
        lr, li = left[:chunk], left[chunk:]
        pair = dot(
            jnp.concatenate(
                [jnp.concatenate([lr, -li], 1), jnp.concatenate([li, lr], 1)], 0),
            zfull[...])
        for owner in range(tc):
            for part in range(2):
                first = part * chunk + owner * cl
                osend[p, owner, part] = pair[first:first + cl].astype(BF16)
        for i in range(1, tc):
            x_copy(p, i).start()

    scatter(0)

    qf_copy().wait_recv()
    j_low = lax.broadcasted_iota(jnp.int32, (vecs, small), 1) * NDIL
    k_low = lax.broadcasted_iota(jnp.int32, (vecs, small), 0)
    spread = ((k_low >= j_low) & (k_low < j_low + NDIL)).astype(F32).astype(BF16)

    def widen(values):
        return jnp.where(keep, dot(spread, values), 0.0).astype(BF16)

    zfull[pl.ds(pl.multiple_of(y * vecs, vecs), vecs), :] = widen(q_f[...])
    zfull[pl.ds(pl.multiple_of((1 - y) * vecs, vecs), vecs), :] = widen(q_fr[...])
    meson_copy.wait()

    def step(p, carry):
        scatter(p)
        finish(p - 1)
        return carry

    lax.fori_loop(1, moments, step, 0)
    finish(moments - 1)

    qy_copy().wait_send()
    qf_copy().wait_send()
    for i in range(1, zc):
        qz_copy(i).wait_send()
    for p in range(moments):
        y_copy(p).wait_send()
        for i in range(1, zc):
            z_copy(p, i).wait_send()
        for i in range(1, tc):
            x_copy(p, i).wait()
    for p in range(moments):
        for owner in range(tc):
            out_ref[p, owner] = xrecv[p, owner]
        out_ref[p, t] = osend[p, t]


def body(solutions, eigvecs, meson, momenta, source_time, dilution):
    times_local, _, colors, sites, cols = solutions.shape
    vecs = eigvecs.shape[4]
    moments = momenta.shape[0]
    sc = lax.axis_size("space")
    tc = lax.axis_size("tm")
    zc = sc // 2
    assert times_local == 1 and sc % 2 == 0
    depth = 2 * colors * sites
    flat = colors * sites
    half = cols // 2
    chunk = cols // sc
    cl = chunk // tc
    small = vecs // NDIL

    space = lax.axis_index("space")
    site = space * sites + jnp.arange(sites, dtype=jnp.int32)
    coordinates = jnp.stack([site % SIDE, site // SIDE % SIDE, site // (SIDE * SIDE)], 0)
    windings = jnp.sum(momenta[:, :, None] * coordinates[None], 1)
    angles = 2.0 * jnp.pi / SIDE * windings.astype(F32)
    angles = jnp.tile(angles, (1, colors))[:, None, :]

    column = np.arange(cols)
    owner, within = column // cl, column % cl
    o_t, o_s = owner // sc, owner % sc
    dst = (((o_s % 2) * zc + o_s // 2) * tc + o_t) * cl + within

    vm = pl.BlockSpec(memory_space=pltpu.VMEM)
    dma = pltpu.SemaphoreType.DMA
    nz, nt = max(zc - 1, 1), max(tc - 1, 1)
    received = pl.pallas_call(
        functools.partial(kernel, zc, tc),
        out_shape=jax.ShapeDtypeStruct((moments, tc, 2, cl, cols), BF16),
        in_specs=[vm, vm, pl.BlockSpec(memory_space=pl.ANY), vm, vm, vm, vm],
        out_specs=vm,
        scratch_shapes=[
            pltpu.VMEM((moments, 2 * vecs, vecs), BF16),
            pltpu.VMEM((2, half, depth), F32),
            pltpu.VMEM((cols, depth), BF16),
            pltpu.VMEM((moments, cols, vecs), BF16),
            pltpu.VMEM((moments, cols, vecs), BF16),
            pltpu.VMEM((moments, cols, vecs), F32),
            pltpu.VMEM((moments, zc, 2, chunk, vecs), BF16),
            pltpu.VMEM((moments, nz, 2, chunk, vecs), BF16),
            pltpu.VMEM((moments, tc, 2, cl, cols), BF16),
            pltpu.VMEM((2, small, cols), BF16),
            pltpu.VMEM((small, cols), BF16),
            pltpu.VMEM((small, cols), BF16),
            pltpu.VMEM((nz, small, cols), BF16),
            pltpu.VMEM((small, cols), BF16),
            pltpu.VMEM((small, cols), BF16),
            pltpu.VMEM((2 * vecs, cols), BF16),
            pltpu.VMEM((moments, tc, 2, cl, cols), BF16),
            dma, dma((moments,)), dma((moments,)),
            dma((moments, nz)), dma((moments, nz)),
            dma((moments, nt)), dma((moments, nt)),
            dma, dma, dma((nz,)), dma((nz,)), dma, dma,
        ],
        compiler_params=pltpu.CompilerParams(
            collective_id=0, has_side_effects=True, vmem_limit_bytes=48 * 1024 * 1024),
    )(
        solutions.reshape(depth, cols),
        eigvecs.reshape(depth, vecs),
        meson.reshape(moments, 2 * vecs, vecs),
        jnp.cos(angles),
        jnp.sin(angles),
        jnp.asarray(dst[None, :], jnp.int32),
        dilution[None, :],
    )

    first = (lax.axis_index("tm") * sc + space) * cl
    mine = lax.dynamic_slice_in_dim(source_time, first, cl)
    wanted = (mine[:, None] + jnp.arange(tc, dtype=jnp.int32)[None, :]) % tc
    wanted = wanted[None, None, :, :, None]
    result = jnp.zeros((moments, 2, cl, tc, cols), F32)
    for time in range(tc):
        result = jnp.where(wanted == time, received[:, time, :, :, None, :].astype(F32), result)
    return result


def solution(mesh):
    return jax.shard_map(
        body,
        mesh=mesh,
        in_specs=(
            P(("cfg", "tm"), None, None, "space", None),
            P(("cfg", "tm"), None, None, "space", None),
            P(None, ("cfg", "tm"), None, None, None),
            P(),
            P(),
            P(),
        ),
        out_specs=P(None, None, ("tm", "space"), "cfg", None),
        check_vma=False,
    )
```

```python
import functools

import jax
import jax.numpy as jnp
import numpy as np
from jax import lax
from jax.experimental import pallas as pl
from jax.experimental.pallas import tpu as pltpu
from jax.sharding import PartitionSpec as P

SIDE = 48
NDIL = 4
MESH = pl.DeviceIdType.MESH
F32 = jnp.float32
BF16 = jnp.bfloat16


def dot(a, b, dims=((1,), (0,))):
    return lax.dot_general(a, b, (dims, ((), ())), preferred_element_type=F32)


def split(values):
    high = values.astype(BF16)
    return high, (values - high.astype(F32)).astype(BF16)


def kernel(
    zc, tc,
    sol_hbm, eig_hbm, meson_hbm, mom_ref, place_ref, dst_ref, dil_ref,
    out_ref,
    sol_ref, eig_ref, meson, cos_ref, sin_ref, solt, lhs, ysend, yrecv, own, ysum, zsend, zrecv, osend,
    q_own, q_sum, q_y, q_yr, q_z, q_zr, q_f, q_fr, zfull, xrecv,
    sol_sem, eig_sem, meson_sem, ys, yr, zs, zr, xs, xr, qys, qyr, qzs, qzr, qfs, qfr,
):
    moments = mom_ref.shape[0]
    depth, cols = sol_hbm.shape
    vecs = eig_hbm.shape[1]
    half = cols // 2
    flat = depth // 2
    chunk = half // zc
    cl = chunk // tc
    small = vecs // NDIL

    s = lax.axis_index("space")
    t = lax.axis_index("tm")
    y = s % 2
    z = s // 2
    ypeer = {"space": z * 2 + (1 - y)}

    def zpeer(i):
        return {"space": ((z + i) % zc) * 2 + y}

    def xpeer(i):
        return (t + i) % tc

    def y_copy(p):
        return pltpu.make_async_remote_copy(
            src_ref=ysend.at[p], dst_ref=yrecv.at[p], send_sem=ys.at[p], recv_sem=yr.at[p],
            device_id=ypeer, device_id_type=MESH)

    def z_copy(p, i):
        return pltpu.make_async_remote_copy(
            src_ref=zsend.at[p, (z + i) % zc], dst_ref=zrecv.at[p, i - 1],
            send_sem=zs.at[p, i - 1], recv_sem=zr.at[p, i - 1],
            device_id=zpeer(i), device_id_type=MESH)

    def x_copy(p, i):
        return pltpu.make_async_remote_copy(
            src_ref=osend.at[p, xpeer(i)], dst_ref=xrecv.at[p, t],
            send_sem=xs.at[p, i - 1], recv_sem=xr.at[p, i - 1],
            device_id={"tm": xpeer(i)}, device_id_type=MESH)

    def qy_copy():
        return pltpu.make_async_remote_copy(
            src_ref=q_y.at[1 - y], dst_ref=q_yr, send_sem=qys, recv_sem=qyr,
            device_id=ypeer, device_id_type=MESH)

    def qz_copy(i):
        return pltpu.make_async_remote_copy(
            src_ref=q_z, dst_ref=q_zr.at[i - 1], send_sem=qzs.at[i - 1], recv_sem=qzr.at[i - 1],
            device_id=zpeer(i), device_id_type=MESH)

    def qf_copy():
        return pltpu.make_async_remote_copy(
            src_ref=q_f, dst_ref=q_fr, send_sem=qfs, recv_sem=qfr,
            device_id=ypeer, device_id_type=MESH)

    sol_copy = pltpu.make_async_copy(sol_hbm, sol_ref, sol_sem)
    sol_copy.start()
    eig_copy = pltpu.make_async_copy(eig_hbm, eig_ref, eig_sem)
    eig_copy.start()
    meson_copy = pltpu.make_async_copy(meson_hbm, meson, meson_sem)
    meson_copy.start()

    barrier = pltpu.get_barrier_semaphore()
    pl.semaphore_signal(barrier, inc=1, device_id=ypeer, device_id_type=MESH)
    for i in range(1, zc):
        pl.semaphore_signal(barrier, inc=1, device_id=zpeer(i), device_id_type=MESH)
    for i in range(1, tc):
        pl.semaphore_signal(barrier, inc=1, device_id={"tm": xpeer(i)}, device_id_type=MESH)

    colors = flat // place_ref.shape[2]
    places = place_ref[s]
    for p in range(moments):
        winding = mom_ref[p, 0] * places[0:1]
        for axis in range(1, 3):
            winding = winding + mom_ref[p, axis] * places[axis:axis + 1]
        angle = 2.0 * jnp.pi / SIDE * winding.astype(F32)
        cos_ref[p] = jnp.concatenate([jnp.cos(angle)] * colors, 1)
        sin_ref[p] = jnp.concatenate([jnp.sin(angle)] * colors, 1)

    sol_copy.wait()
    eig_copy.wait()
    sol = sol_ref[...]
    eig = eig_ref[...]
    turned = jnp.concatenate([sol[flat:], -sol[:flat]], 0)
    k_row = lax.broadcasted_iota(jnp.int32, (vecs, cols), 0)
    keep = (k_row & (NDIL - 1)) == dil_ref[...].reshape(1, cols)
    j_row = lax.broadcasted_iota(jnp.int32, (small, vecs), 0) * NDIL
    k_col = lax.broadcasted_iota(jnp.int32, (small, vecs), 1)
    gather = ((k_col >= j_row) & (k_col < j_row + NDIL)).astype(F32).astype(BF16)
    for part, rhs in enumerate((sol, turned)):
        full = dot(eig, rhs, ((0,), (0,)))
        high, low = split(jnp.where(keep, full, 0.0))
        packed = dot(gather, high) + dot(gather, low)
        q_own[part] = packed
        q_y[part] = packed.astype(BF16)

    c_row = lax.broadcasted_iota(jnp.int32, (cols, cols), 0)
    perm = (c_row == dst_ref[...]).astype(F32).astype(BF16)
    moved = dot(perm, sol, ((1,), (1,)))
    solt[0] = moved[:half]
    solt[1] = moved[half:]

    pl.semaphore_wait(barrier, 1 + (zc - 1) + (tc - 1))
    qy_copy().start()

    def partial(p, which):
        block = solt[which]
        re, im = block[:, :flat], block[:, flat:]
        c, sn = cos_ref[p], sin_ref[p]
        pr = (c * re + sn * im).astype(BF16)
        pi = (c * im - sn * re).astype(BF16)
        lhs[:half, :flat] = pr
        lhs[:half, flat:] = pi
        lhs[half:, :flat] = pi
        lhs[half:, flat:] = -pr
        return dot(lhs[...], eig_ref[...])

    def send_other(p, carry):
        ysend[p] = partial(p, 1 - y).astype(BF16)
        y_copy(p).start()
        return carry

    lax.fori_loop(0, moments, send_other, 0)

    qy_copy().wait_recv()
    q_sum[...] = q_own[y] + q_yr[...].astype(F32)
    q_z[...] = q_sum[...].astype(BF16)
    for i in range(1, zc):
        qz_copy(i).start()

    def keep_own(p, carry):
        own[p] = partial(p, y)
        return carry

    lax.fori_loop(0, moments, keep_own, 0)

    for i in range(1, zc):
        qz_copy(i).wait_recv()
    total = q_sum[...]
    for i in range(1, zc):
        total = total + q_zr[i - 1].astype(F32)
    q_f[...] = total.astype(BF16)
    qf_copy().start()

    def scatter(p):
        y_copy(p).wait_recv()
        for c in range(zc):
            for part in range(2):
                rows = pl.ds(part * half + c * chunk, chunk)
                summed = own[p, rows] + yrecv[p, rows].astype(F32)
                ysum[p, c, part] = summed
                zsend[p, c, part] = summed.astype(BF16)
        for i in range(1, zc):
            z_copy(p, i).start()

    def finish(p):
        coef = ysum[p, z]
        for i in range(1, zc):
            z_copy(p, i).wait_recv()
            coef = coef + zrecv[p, i - 1].astype(F32)
        cr, ci = coef[0], coef[1]
        rows = 2 * chunk
        both = split(jnp.concatenate(
            [jnp.concatenate([cr, ci], 1), jnp.concatenate([-ci, cr], 1)], 0))
        left = dot(jnp.concatenate(both, 0), meson[p])
        left = left[:rows] + left[rows:]
        lr, li = left[:chunk], left[chunk:]
        both = split(jnp.concatenate(
            [jnp.concatenate([lr, -li], 1), jnp.concatenate([li, lr], 1)], 0))
        pair = dot(jnp.concatenate(both, 0), zfull[...])
        pair = pair[:rows] + pair[rows:]
        for owner in range(tc):
            for part in range(2):
                first = part * chunk + owner * cl
                osend[p, owner, part] = pair[first:first + cl].astype(BF16)
        for i in range(1, tc):
            x_copy(p, i).start()

    scatter(0)

    qf_copy().wait_recv()
    j_low = lax.broadcasted_iota(jnp.int32, (vecs, small), 1) * NDIL
    k_low = lax.broadcasted_iota(jnp.int32, (vecs, small), 0)
    spread = ((k_low >= j_low) & (k_low < j_low + NDIL)).astype(F32).astype(BF16)

    def widen(values):
        return jnp.where(keep, dot(spread, values), 0.0).astype(BF16)

    zfull[pl.ds(pl.multiple_of(y * vecs, vecs), vecs), :] = widen(q_f[...])
    zfull[pl.ds(pl.multiple_of((1 - y) * vecs, vecs), vecs), :] = widen(q_fr[...])
    meson_copy.wait()

    def step(p, carry):
        scatter(p)
        finish(p - 1)
        return carry

    lax.fori_loop(1, moments, step, 0)
    finish(moments - 1)

    qy_copy().wait_send()
    qf_copy().wait_send()
    for i in range(1, zc):
        qz_copy(i).wait_send()
    for p in range(moments):
        y_copy(p).wait_send()
        for i in range(1, zc):
            z_copy(p, i).wait_send()
        for i in range(1, tc):
            x_copy(p, i).wait()
    for p in range(moments):
        for owner in range(tc):
            out_ref[p, owner] = xrecv[p, owner]
        out_ref[p, t] = osend[p, t]


def body(solutions, eigvecs, meson, momenta, source_time, dilution):
    times_local, _, colors, sites, cols = solutions.shape
    vecs = eigvecs.shape[4]
    moments = momenta.shape[0]
    sc = lax.axis_size("space")
    tc = lax.axis_size("tm")
    zc = sc // 2
    assert times_local == 1 and sc % 2 == 0
    depth = 2 * colors * sites
    flat = colors * sites
    half = cols // 2
    chunk = cols // sc
    cl = chunk // tc
    small = vecs // NDIL

    space = lax.axis_index("space")
    site = np.arange(sc * sites).reshape(sc, 1, sites)
    places = np.concatenate([site % SIDE, site // SIDE % SIDE, site // (SIDE * SIDE)], 1)

    column = np.arange(cols)
    owner, within = column // cl, column % cl
    o_t, o_s = owner // sc, owner % sc
    dst = (((o_s % 2) * zc + o_s // 2) * tc + o_t) * cl + within

    vm = pl.BlockSpec(memory_space=pltpu.VMEM)
    hbm = pl.BlockSpec(memory_space=pltpu.HBM)
    dma = pltpu.SemaphoreType.DMA
    nz, nt = max(zc - 1, 1), max(tc - 1, 1)
    received = pl.pallas_call(
        functools.partial(kernel, zc, tc),
        out_shape=jax.ShapeDtypeStruct((moments, tc, 2, cl, cols), BF16),
        in_specs=[hbm, hbm, hbm, pl.BlockSpec(memory_space=pltpu.SMEM), vm, vm, vm],
        out_specs=vm,
        scratch_shapes=[
            pltpu.VMEM((depth, cols), BF16),
            pltpu.VMEM((depth, vecs), BF16),
            pltpu.VMEM((moments, 2 * vecs, vecs), BF16),
            pltpu.VMEM((moments, 1, flat), F32),
            pltpu.VMEM((moments, 1, flat), F32),
            pltpu.VMEM((2, half, depth), F32),
            pltpu.VMEM((cols, depth), BF16),
            pltpu.VMEM((moments, cols, vecs), BF16),
            pltpu.VMEM((moments, cols, vecs), BF16),
            pltpu.VMEM((moments, cols, vecs), F32),
            pltpu.VMEM((moments, zc, 2, chunk, vecs), F32),
            pltpu.VMEM((moments, zc, 2, chunk, vecs), BF16),
            pltpu.VMEM((moments, nz, 2, chunk, vecs), BF16),
            pltpu.VMEM((moments, tc, 2, cl, cols), BF16),
            pltpu.VMEM((2, small, cols), F32),
            pltpu.VMEM((small, cols), F32),
            pltpu.VMEM((2, small, cols), BF16),
            pltpu.VMEM((small, cols), BF16),
            pltpu.VMEM((small, cols), BF16),
            pltpu.VMEM((nz, small, cols), BF16),
            pltpu.VMEM((small, cols), BF16),
            pltpu.VMEM((small, cols), BF16),
            pltpu.VMEM((2 * vecs, cols), BF16),
            pltpu.VMEM((moments, tc, 2, cl, cols), BF16),
            dma, dma, dma, dma((moments,)), dma((moments,)),
            dma((moments, nz)), dma((moments, nz)),
            dma((moments, nt)), dma((moments, nt)),
            dma, dma, dma((nz,)), dma((nz,)), dma, dma,
        ],
        compiler_params=pltpu.CompilerParams(
            collective_id=0, has_side_effects=True),
    )(
        solutions.reshape(depth, cols),
        eigvecs.reshape(depth, vecs),
        meson.reshape(moments, 2 * vecs, vecs),
        momenta,
        jnp.asarray(places, jnp.int32),
        jnp.asarray(dst[None, :], jnp.int32),
        dilution,
    )

    first = (lax.axis_index("tm") * sc + space) * cl
    mine = lax.dynamic_slice_in_dim(source_time, first, cl)
    wanted = (mine[:, None] + jnp.arange(tc, dtype=jnp.int32)[None, :]) % tc
    wanted = wanted[None, None, :, :, None]
    result = jnp.zeros((moments, 2, cl, tc, cols), F32)
    for time in range(tc):
        result = jnp.where(wanted == time, received[:, time, :, :, None, :].astype(F32), result)
    return result


def solution(mesh):
    return jax.shard_map(
        body,
        mesh=mesh,
        in_specs=(
            P(("cfg", "tm"), None, None, "space", None),
            P(("cfg", "tm"), None, None, "space", None),
            P(None, ("cfg", "tm"), None, None, None),
            P(),
            P(),
            P(),
        ),
        out_specs=P(None, None, ("tm", "space"), "cfg", None),
        check_vma=False,
    )
```

```python
import functools

import jax
import jax.numpy as jnp
import numpy as np
from jax import lax
from jax.experimental import pallas as pl
from jax.experimental.pallas import tpu as pltpu
from jax.sharding import PartitionSpec as P

SIDE = 48
NDIL = 4
MESH = pl.DeviceIdType.MESH
F32 = jnp.float32
BF16 = jnp.bfloat16


def dot(a, b, dims=((1,), (0,))):
    return lax.dot_general(a, b, (dims, ((), ())), preferred_element_type=F32)


def split(values):
    high = values.astype(BF16)
    return high, (values - high.astype(F32)).astype(BF16)


def kernel(
    zc, tc,
    sol_hbm, eig_hbm, meson_hbm, mom_ref, place_ref, dst_ref, dil_ref,
    out_ref,
    sol_ref, eig_ref, meson, cos_ref, sin_ref, solt, lhs, ysend, yrecv, own,
    ysum, zsend, zrecv, osend, xrecv,
    q_own, q_sum, q_y, q_yr, q_z, q_zr, q_f, q_fr, zfull,
    sol_sem, eig_sem, meson_sem, ys, yr, zs, zr, xs, xr,
    qys, qyr, qzs, qzr, qas, qar, qfs, qfr,
):
    moments = mom_ref.shape[0]
    depth, cols = sol_hbm.shape
    vecs = eig_hbm.shape[1]
    flat = depth // 2
    pieces = 2 * moments
    low_count = tc // 2
    cl = cols // (2 * zc * tc)
    sub = low_count * cl
    prow = zc * sub
    small = vecs // NDIL
    q_rows = small // zc

    s = lax.axis_index("space")
    t = lax.axis_index("tm")
    y = s % 2
    z = s // 2
    group = t // low_count
    low = t % low_count
    ypeer = {"space": z * 2 + (1 - y)}

    def zpeer(i):
        return {"space": ((z + i) % zc) * 2 + y}

    def y_copy(n):
        return pltpu.make_async_remote_copy(
            src_ref=ysend.at[n], dst_ref=yrecv.at[n], send_sem=ys.at[n], recv_sem=yr.at[n],
            device_id=ypeer, device_id_type=MESH)

    def z_copy(n, i):
        return pltpu.make_async_remote_copy(
            src_ref=zsend.at[n, (z + i) % zc], dst_ref=zrecv.at[n, i - 1],
            send_sem=zs.at[n, i - 1], recv_sem=zr.at[n, i - 1],
            device_id=zpeer(i), device_id_type=MESH)

    def x_copy(p, cross, i):
        side = 1 - group if cross else group
        peer = side * low_count + (low + i) % low_count
        slot = i if cross else low_count + i
        return pltpu.make_async_remote_copy(
            src_ref=osend.at[p, peer], dst_ref=xrecv.at[p, t],
            send_sem=xs.at[p, slot], recv_sem=xr.at[p, slot],
            device_id={"tm": peer}, device_id_type=MESH)

    def qy_copy():
        return pltpu.make_async_remote_copy(
            src_ref=q_y.at[1 - y], dst_ref=q_yr, send_sem=qys, recv_sem=qyr,
            device_id=ypeer, device_id_type=MESH)

    def qz_copy(i):
        return pltpu.make_async_remote_copy(
            src_ref=q_z.at[(z + i) % zc], dst_ref=q_zr.at[i - 1],
            send_sem=qzs.at[i - 1], recv_sem=qzr.at[i - 1],
            device_id=zpeer(i), device_id_type=MESH)

    def qa_copy(i):
        return pltpu.make_async_remote_copy(
            src_ref=q_f.at[z], dst_ref=q_f.at[z],
            send_sem=qas.at[i - 1], recv_sem=qar.at[i - 1],
            device_id=zpeer(i), device_id_type=MESH)

    def qf_copy():
        return pltpu.make_async_remote_copy(
            src_ref=q_f, dst_ref=q_fr, send_sem=qfs, recv_sem=qfr,
            device_id=ypeer, device_id_type=MESH)

    sol_copy = pltpu.make_async_copy(sol_hbm, sol_ref, sol_sem)
    sol_copy.start()
    eig_copy = pltpu.make_async_copy(eig_hbm, eig_ref, eig_sem)
    eig_copy.start()
    meson_copy = pltpu.make_async_copy(meson_hbm, meson, meson_sem)
    meson_copy.start()

    barrier = pltpu.get_barrier_semaphore()
    pl.semaphore_signal(barrier, inc=1, device_id=ypeer, device_id_type=MESH)
    for i in range(1, zc):
        pl.semaphore_signal(barrier, inc=1, device_id=zpeer(i), device_id_type=MESH)
    for i in range(1, tc):
        pl.semaphore_signal(
            barrier, inc=1, device_id={"tm": (t + i) % tc}, device_id_type=MESH)

    colors = flat // place_ref.shape[2]
    places = place_ref[s]
    for p in range(moments):
        winding = mom_ref[p, 0] * places[0:1]
        for axis in range(1, 3):
            winding = winding + mom_ref[p, axis] * places[axis:axis + 1]
        angle = 2.0 * jnp.pi / SIDE * winding.astype(F32)
        cos_ref[p] = jnp.concatenate([jnp.cos(angle)] * colors, 1)
        sin_ref[p] = jnp.concatenate([jnp.sin(angle)] * colors, 1)

    c_row = lax.broadcasted_iota(jnp.int32, (cols, cols), 0)
    perm = (c_row == dst_ref[...]).astype(F32).astype(BF16)
    sol_copy.wait()
    moved = dot(perm, sol_ref[...], ((1,), (1,)))
    for block in range(4):
        solt[block] = moved[block * prow:(block + 1) * prow]
    eig_copy.wait()

    def partial(n, which):
        p = n // 2
        block = solt[which * 2 + (group + 1 + n) % 2]
        re, im = block[:, :flat], block[:, flat:]
        c, sn = cos_ref[p], sin_ref[p]
        pr = (c * re + sn * im).astype(BF16)
        pi = (c * im - sn * re).astype(BF16)
        lhs[:prow, :flat] = pr
        lhs[:prow, flat:] = pi
        lhs[prow:, :flat] = pi
        lhs[prow:, flat:] = -pr
        return dot(lhs[...], eig_ref[...])

    def send_other(n, carry):
        ysend[n] = partial(n, 1 - y).astype(BF16)
        y_copy(n).start()
        return carry

    def keep_own(n, carry):
        own[n] = partial(n, y)
        return carry

    def scatter(n, carry):
        y_copy(n).wait_recv()
        for c in range(zc):
            for part in range(2):
                rows = pl.ds(part * prow + c * sub, sub)
                summed = own[n, rows] + yrecv[n, rows].astype(F32)
                ysum[n, c, part] = summed
                zsend[n, c, part] = summed.astype(BF16)
        for i in range(1, zc):
            z_copy(n, i).start()
        return carry

    def finish(n, carry):
        p = n // 2
        side = (group + 1 + n) % 2
        coef = ysum[n, z]
        for i in range(1, zc):
            z_copy(n, i).wait_recv()
            coef = coef + zrecv[n, i - 1].astype(F32)
        cr, ci = coef[0], coef[1]
        rows = 2 * sub
        both = split(jnp.concatenate(
            [jnp.concatenate([cr, ci], 1), jnp.concatenate([-ci, cr], 1)], 0))
        left = dot(jnp.concatenate(both, 0), meson[p])
        left = left[:rows] + left[rows:]
        lr, li = left[:sub], left[sub:]
        both = split(jnp.concatenate(
            [jnp.concatenate([lr, -li], 1), jnp.concatenate([li, lr], 1)], 0))
        pair = dot(jnp.concatenate(both, 0), zfull[...])
        pair = pair[:rows] + pair[rows:]
        for owner in range(low_count):
            for part in range(2):
                first = part * sub + owner * cl
                osend[p, side * low_count + owner, part] = pair[first:first + cl].astype(BF16)

        @pl.when(n % 2 == 0)
        def _():
            for i in range(low_count):
                x_copy(p, True, i).start()

        if low_count > 1:
            @pl.when(n % 2 == 1)
            def _():
                for i in range(1, low_count):
                    x_copy(p, False, i).start()

        return carry

    def run(stage, first, last):
        lax.fori_loop(first, last, stage, 0)

    pl.semaphore_wait(barrier, 1 + (zc - 1) + (tc - 1))
    run(send_other, 0, 1)

    sol = sol_ref[...]
    eig = eig_ref[...]
    turned = jnp.concatenate([sol[flat:], -sol[:flat]], 0)
    k_row = lax.broadcasted_iota(jnp.int32, (vecs, cols), 0)
    keep = (k_row & (NDIL - 1)) == dil_ref[...].reshape(1, cols)
    j_row = lax.broadcasted_iota(jnp.int32, (small, vecs), 0) * NDIL
    k_col = lax.broadcasted_iota(jnp.int32, (small, vecs), 1)
    gather = ((k_col >= j_row) & (k_col < j_row + NDIL)).astype(F32).astype(BF16)
    for part, rhs in enumerate((sol, turned)):
        full = dot(eig, rhs, ((0,), (0,)))
        high, rest = split(jnp.where(keep, full, 0.0))
        packed = dot(gather, high) + dot(gather, rest)
        q_own[part] = packed
        q_y[part] = packed.astype(BF16)
    qy_copy().start()

    run(send_other, 1, 3)

    qy_copy().wait_recv()
    for c in range(zc):
        rows = pl.ds(c * q_rows, q_rows)
        summed = q_own[y, rows] + q_yr[rows].astype(F32)
        q_sum[c] = summed
        q_z[c] = summed.astype(BF16)
    for i in range(1, zc):
        qz_copy(i).start()

    run(send_other, 3, 5)
    run(keep_own, 0, 2)
    run(scatter, 0, 1)

    for i in range(1, zc):
        qz_copy(i).wait_recv()
    total = q_sum[z]
    for i in range(1, zc):
        total = total + q_zr[i - 1].astype(F32)
    q_f[z] = total.astype(BF16)
    for i in range(1, zc):
        qa_copy(i).start()

    run(keep_own, 2, 4)
    run(scatter, 1, 2)
    for i in range(1, zc):
        qa_copy(i).wait_recv()
    qf_copy().start()

    run(send_other, 5, pieces)
    run(scatter, 2, 3)
    run(keep_own, 4, pieces)
    run(scatter, 3, 4)

    qf_copy().wait_recv()
    j_low = lax.broadcasted_iota(jnp.int32, (vecs, small), 1) * NDIL
    k_low = lax.broadcasted_iota(jnp.int32, (vecs, small), 0)
    spread = ((k_low >= j_low) & (k_low < j_low + NDIL)).astype(F32).astype(BF16)

    def widen(ref):
        values = jnp.concatenate([ref[c].astype(F32) for c in range(zc)], 0).astype(BF16)
        return jnp.where(keep, dot(spread, values), 0.0).astype(BF16)

    zfull[pl.ds(pl.multiple_of(y * vecs, vecs), vecs), :] = widen(q_f)
    zfull[pl.ds(pl.multiple_of((1 - y) * vecs, vecs), vecs), :] = widen(q_fr)
    meson_copy.wait()

    def step(n, carry):
        scatter(n, 0)
        finish(n - 4, 0)
        return carry

    run(step, 4, pieces)
    run(finish, pieces - 4, pieces)

    qy_copy().wait_send()
    qf_copy().wait_send()
    for i in range(1, zc):
        qz_copy(i).wait_send()
        qa_copy(i).wait_send()

    def drain(n, carry):
        y_copy(n).wait_send()
        for i in range(1, zc):
            z_copy(n, i).wait_send()
        return carry

    run(drain, 0, pieces)
    for p in range(moments):
        for i in range(low_count):
            x_copy(p, True, i).wait()
        for i in range(1, low_count):
            x_copy(p, False, i).wait()
        for owner in range(tc):
            out_ref[p, owner] = xrecv[p, owner]
        out_ref[p, t] = osend[p, t]


def body(solutions, eigvecs, meson, momenta, source_time, dilution):
    times_local, _, colors, sites, cols = solutions.shape
    vecs = eigvecs.shape[4]
    moments = momenta.shape[0]
    sc = lax.axis_size("space")
    tc = lax.axis_size("tm")
    zc = sc // 2
    assert times_local == 1 and sc % 2 == 0 and tc % 2 == 0 and moments >= 3
    depth = 2 * colors * sites
    flat = colors * sites
    cl = cols // (sc * tc)
    low_count = tc // 2
    sub = low_count * cl
    prow = zc * sub
    pieces = 2 * moments
    small = vecs // NDIL
    q_rows = small // zc

    space = lax.axis_index("space")
    site = np.arange(sc * sites).reshape(sc, 1, sites)
    places = np.concatenate([site % SIDE, site // SIDE % SIDE, site // (SIDE * SIDE)], 1)

    column = np.arange(cols)
    owner, within = column // cl, column % cl
    o_t, o_s = owner // sc, owner % sc
    block = (o_s % 2) * 2 + o_t // low_count
    dst = ((block * zc + o_s // 2) * low_count + o_t % low_count) * cl + within

    vm = pl.BlockSpec(memory_space=pltpu.VMEM)
    hbm = pl.BlockSpec(memory_space=pltpu.HBM)
    dma = pltpu.SemaphoreType.DMA
    nz = max(zc - 1, 1)
    received = pl.pallas_call(
        functools.partial(kernel, zc, tc),
        out_shape=jax.ShapeDtypeStruct((moments, tc, 2, cl, cols), BF16),
        in_specs=[hbm, hbm, hbm, pl.BlockSpec(memory_space=pltpu.SMEM), vm, vm, vm],
        out_specs=vm,
        scratch_shapes=[
            pltpu.VMEM((depth, cols), BF16),
            pltpu.VMEM((depth, vecs), BF16),
            pltpu.VMEM((moments, 2 * vecs, vecs), BF16),
            pltpu.VMEM((moments, 1, flat), F32),
            pltpu.VMEM((moments, 1, flat), F32),
            pltpu.VMEM((4, prow, depth), F32),
            pltpu.VMEM((2 * prow, depth), BF16),
            pltpu.VMEM((pieces, 2 * prow, vecs), BF16),
            pltpu.VMEM((pieces, 2 * prow, vecs), BF16),
            pltpu.VMEM((pieces, 2 * prow, vecs), F32),
            pltpu.VMEM((pieces, zc, 2, sub, vecs), F32),
            pltpu.VMEM((pieces, zc, 2, sub, vecs), BF16),
            pltpu.VMEM((pieces, nz, 2, sub, vecs), BF16),
            pltpu.VMEM((moments, tc, 2, cl, cols), BF16),
            pltpu.VMEM((moments, tc, 2, cl, cols), BF16),
            pltpu.VMEM((2, small, cols), F32),
            pltpu.VMEM((zc, q_rows, cols), F32),
            pltpu.VMEM((2, small, cols), BF16),
            pltpu.VMEM((small, cols), BF16),
            pltpu.VMEM((zc, q_rows, cols), BF16),
            pltpu.VMEM((nz, q_rows, cols), BF16),
            pltpu.VMEM((zc, q_rows, cols), BF16),
            pltpu.VMEM((zc, q_rows, cols), BF16),
            pltpu.VMEM((2 * vecs, cols), BF16),
            dma, dma, dma,
            dma((pieces,)), dma((pieces,)),
            dma((pieces, nz)), dma((pieces, nz)),
            dma((moments, tc)), dma((moments, tc)),
            dma, dma, dma((nz,)), dma((nz,)), dma((nz,)), dma((nz,)), dma, dma,
        ],
        compiler_params=pltpu.CompilerParams(
            collective_id=0, has_side_effects=True),
    )(
        solutions.reshape(depth, cols),
        eigvecs.reshape(depth, vecs),
        meson.reshape(moments, 2 * vecs, vecs),
        momenta,
        jnp.asarray(places, jnp.int32),
        jnp.asarray(dst[None, :], jnp.int32),
        dilution,
    )

    first = (lax.axis_index("tm") * sc + space) * cl
    mine = lax.dynamic_slice_in_dim(source_time, first, cl)
    wanted = (mine[:, None] + jnp.arange(tc, dtype=jnp.int32)[None, :]) % tc
    wanted = wanted[None, None, :, :, None]
    result = jnp.zeros((moments, 2, cl, tc, cols), F32)
    for time in range(tc):
        result = jnp.where(wanted == time, received[:, time, :, :, None, :].astype(F32), result)
    return result


def solution(mesh):
    return jax.shard_map(
        body,
        mesh=mesh,
        in_specs=(
            P(("cfg", "tm"), None, None, "space", None),
            P(("cfg", "tm"), None, None, "space", None),
            P(None, ("cfg", "tm"), None, None, None),
            P(),
            P(),
            P(),
        ),
        out_specs=P(None, None, ("tm", "space"), "cfg", None),
        check_vma=False,
    )
```
